32 devices in a mesh: dp: 16 (over z, y, x), tensor: 2 (over core).
Axes of the slice: x: 2, y: 2, z: 4, core: 2. Of those that a mesh axis runs over, the one named last changes fastest.
Arguments:
- block_input: float32 [8192, 768], P(('dp', 'tensor')), may hold values from -6 to 6
- cotangent: float32 [8192, 768], P(('dp', 'tensor')), may hold values from -6 to 6
- segment_ids: int32 [8192], P('dp'), may hold values from 0 to 63, as said below
- positions: int32 [8192], P('dp'), may hold values from 0 to 511, as said below
- heads_weight: float32 [768, 3, 768], P('dp', None, 'tensor')
- heads_weight_first: float32 [768, 3, 768], P('dp', None, 'tensor'), may hold values from -64 to 64
- heads_weight_second: float32 [768, 3, 768], P('dp', None, 'tensor'), may hold values from 20 to 2000
- output_weight: float32 [768, 768], P(('tensor', 'dp')), may hold values from -0.875 to 0.875
- output_weight_first: float32 [768, 768], P(('tensor', 'dp')), may hold values from -64 to 64
- output_weight_second: float32 [768, 768], P(('tensor', 'dp')), may hold values from 20 to 2000
- expand_weight: float32 [768, 3072], P('dp', 'tensor'), may hold values from -0.21875 to 0.21875
- expand_weight_first: float32 [768, 3072], P('dp', 'tensor'), may hold values from -64 to 64
- expand_weight_second: float32 [768, 3072], P('dp', 'tensor'), may hold values from 20 to 2000
- shrink_weight: float32 [3072, 768], P(('tensor', 'dp')), may hold values from -0.109375 to 0.109375
- shrink_weight_first: float32 [3072, 768], P(('tensor', 'dp')), may hold values from -64 to 64
- shrink_weight_second: float32 [3072, 768], P(('tensor', 'dp')), may hold values from 20 to 2000
- attention_gain: float32 [768], P(('dp', 'tensor')), may hold values from 0.5 to 1.5
- attention_gain_first: float32 [768], P(('dp', 'tensor')), may hold values from -192 to 192
- attention_gain_second: float32 [768], P(('dp', 'tensor')), may hold values from 100 to 10000
- attention_shift: float32 [768], P(('dp', 'tensor')), may hold values from -1.75 to 1.75
- attention_shift_first: float32 [768], P(('dp', 'tensor')), may hold values from -192 to 192
- attention_shift_second: float32 [768], P(('dp', 'tensor')), may hold values from 100 to 10000
- feedforward_gain: float32 [768], P(('dp', 'tensor')), may hold values from 0.5 to 1.5
- feedforward_gain_first: float32 [768], P(('dp', 'tensor')), may hold values from -192 to 192
- feedforward_gain_second: float32 [768], P(('dp', 'tensor')), may hold values from 100 to 10000
- feedforward_shift: float32 [768], P(('dp', 'tensor')), may hold values from -1.75 to 1.75
- feedforward_shift_first: float32 [768], P(('dp', 'tensor')), may hold values from -192 to 192
- feedforward_shift_second: float32 [768], P(('dp', 'tensor')), may hold values from 100 to 10000
- heads_bias: float32 [2304], P(('dp', 'tensor')), may hold values from -1.75 to 1.75
- heads_bias_first: float32 [2304], P(('dp', 'tensor')), may hold values from -192 to 192
- heads_bias_second: float32 [2304], P(('dp', 'tensor')), may hold values from 100 to 10000
- output_bias: float32 [768], P(('dp', 'tensor')), may hold values from -1.75 to 1.75
- output_bias_first: float32 [768], P(('dp', 'tensor')), may hold values from -192 to 192
- output_bias_second: float32 [768], P(('dp', 'tensor')), may hold values from 100 to 10000
- expand_bias: float32 [3072], P(('dp', 'tensor')), may hold values from -1.75 to 1.75
- expand_bias_first: float32 [3072], P(('dp', 'tensor')), may hold values from -192 to 192
- expand_bias_second: float32 [3072], P(('dp', 'tensor')), may hold values from 100 to 10000
- shrink_bias: float32 [768], P(('dp', 'tensor')), may hold values from -1.75 to 1.75
- shrink_bias_first: float32 [768], P(('dp', 'tensor')), may hold values from -192 to 192
- shrink_bias_second: float32 [768], P(('dp', 'tensor')), may hold values from 100 to 10000
Outputs:
- block_output: float32 [8192, 768], P(('dp', 'tensor'))
- input_gradient: float32 [8192, 768], P(('dp', 'tensor'))
- heads_weight_gradient: float32 [768, 3, 768], P('dp', None, 'tensor')
- heads_weight_next: float32 [768, 3, 768], P('dp', None, 'tensor')
- heads_weight_first_next: float32 [768, 3, 768], P('dp', None, 'tensor')
- heads_weight_second_next: float32 [768, 3, 768], P('dp', None, 'tensor')
- output_weight_gradient: float32 [768, 768], P(('tensor', 'dp'))
- output_weight_next: float32 [768, 768], P(('tensor', 'dp'))
- output_weight_first_next: float32 [768, 768], P(('tensor', 'dp'))
- output_weight_second_next: float32 [768, 768], P(('tensor', 'dp'))
- expand_weight_gradient: float32 [768, 3072], P('dp', 'tensor')
- expand_weight_next: float32 [768, 3072], P('dp', 'tensor')
- expand_weight_first_next: float32 [768, 3072], P('dp', 'tensor')
- expand_weight_second_next: float32 [768, 3072], P('dp', 'tensor')
- shrink_weight_gradient: float32 [3072, 768], P(('tensor', 'dp'))
- shrink_weight_next: float32 [3072, 768], P(('tensor', 'dp'))
- shrink_weight_first_next: float32 [3072, 768], P(('tensor', 'dp'))
- shrink_weight_second_next: float32 [3072, 768], P(('tensor', 'dp'))
- attention_gain_gradient: float32 [768], P(('dp', 'tensor'))
- attention_gain_next: float32 [768], P(('dp', 'tensor'))
- attention_gain_first_next: float32 [768], P(('dp', 'tensor'))
- attention_gain_second_next: float32 [768], P(('dp', 'tensor'))
- attention_shift_gradient: float32 [768], P(('dp', 'tensor'))
- attention_shift_next: float32 [768], P(('dp', 'tensor'))
- attention_shift_first_next: float32 [768], P(('dp', 'tensor'))
- attention_shift_second_next: float32 [768], P(('dp', 'tensor'))
- feedforward_gain_gradient: float32 [768], P(('dp', 'tensor'))
- feedforward_gain_next: float32 [768], P(('dp', 'tensor'))
- feedforward_gain_first_next: float32 [768], P(('dp', 'tensor'))
- feedforward_gain_second_next: float32 [768], P(('dp', 'tensor'))
- feedforward_shift_gradient: float32 [768], P(('dp', 'tensor'))
- feedforward_shift_next: float32 [768], P(('dp', 'tensor'))
- feedforward_shift_first_next: float32 [768], P(('dp', 'tensor'))
- feedforward_shift_second_next: float32 [768], P(('dp', 'tensor'))
- heads_bias_gradient: float32 [2304], P(('dp', 'tensor'))
- heads_bias_next: float32 [2304], P(('dp', 'tensor'))
- heads_bias_first_next: float32 [2304], P(('dp', 'tensor'))
- heads_bias_second_next: float32 [2304], P(('dp', 'tensor'))
- output_bias_gradient: float32 [768], P(('dp', 'tensor'))
- output_bias_next: float32 [768], P(('dp', 'tensor'))
- output_bias_first_next: float32 [768], P(('dp', 'tensor'))
- output_bias_second_next: float32 [768], P(('dp', 'tensor'))
- expand_bias_gradient: float32 [3072], P(('dp', 'tensor'))
- expand_bias_next: float32 [3072], P(('dp', 'tensor'))
- expand_bias_first_next: float32 [3072], P(('dp', 'tensor'))
- expand_bias_second_next: float32 [3072], P(('dp', 'tensor'))
- shrink_bias_gradient: float32 [768], P(('dp', 'tensor'))
- shrink_bias_next: float32 [768], P(('dp', 'tensor'))
- shrink_bias_first_next: float32 [768], P(('dp', 'tensor'))
- shrink_bias_second_next: float32 [768], P(('dp', 'tensor'))
The draws below stay inside these ranges and needn't reach their ends.
Inputs may be any that keep to these rules, and one draw needn't show every extreme that they name: `segment_ids`: within each block of 512 tokens the ids start at 0 and rise by one at each new document; documents never cross blocks and start only at offsets in the block that are multiples of 8. `positions`: each token's offset from the first token of its document.
All inputs are finite; a program needn't handle non-finite values.
Results may differ from the reference program's by a relative error of at most 0.011.
Values may be sent and summed in bfloat16 or wider, within the bound.
No kernel may reach another device: no remote copies, remote signals or barrier semaphores. Data moves between devices by JAX's collectives and lax.ppermute only.
A program may use at most 128 MiB of HBM per device.

```python
import math
import jax
import jax.numpy as jnp
from jax import lax

D = 768
HD = 64
RD = 16
FF = 3072
TOK_DEV = 512
ADAM_STEP = 3
TOKENS = 8192


def document_layout(key):
    keyed = jax.random.fold_in(key, 5)
    packs = TOKENS // TOK_DEV
    coins = jax.random.randint(keyed, (packs, TOK_DEV), 0, 12)
    places = jnp.arange(TOK_DEV, dtype=jnp.int32)[None, :]
    pack_index = jnp.arange(packs, dtype=jnp.int32)[:, None]
    candidate = places % 8 == 0
    chosen = (coins == 0) & (pack_index > 0) | (pack_index == packs - 1)
    starts = candidate & chosen | (places == 0)
    ids = jnp.cumsum(starts.astype(jnp.int32), axis=1) - 1
    first = lax.cummax(jnp.where(starts, places, 0), axis=1)
    offsets = places - first
    return (ids.reshape(-1).astype(jnp.int32), offsets.reshape(-1).astype(jnp.int32))


def draw_segment_ids(key, part):
    return document_layout(key)[0]


def draw_positions(key, part):
    return document_layout(key)[1]


def draw_heads_weight(key, part):
    return jax.random.normal(key, (D, 3, D), jnp.float32) * D ** (-0.5)


def block_scale(own_key, shape, pieces, low, high):
    gain, own = 1.0, jax.random.fold_in(own_key, 6)
    for dim, shards_of in pieces:
        heights = jnp.exp(jax.random.uniform(jax.random.fold_in(own, dim), (shards_of,), jnp.float32, low / len(pieces), high / len(pieces)))
        gain = gain * jnp.repeat(heights, shape[dim] // shards_of).reshape([-1 if axis == dim else 1 for axis in range(len(shape))])
    return gain


def gaussian(own_key, dims, scale, reach, pieces=(), kind=jnp.bfloat16):
    result = jax.random.normal(own_key, dims, jnp.float32) * scale
    if len(pieces) > 0:
        result = block_scale(own_key, dims, pieces, -0.22, 0.18) * result
    return jnp.clip(result, min=-reach, max=reach).astype(kind)


def setup_inputs(seed: int = 0) -> dict:
    streams_of = jax.random.split(jax.random.key(seed), 41)
    block_input = gaussian(streams_of[0], (TOKENS, D), 1.0, 6.0, ((0, 32),), jnp.float32)
    cotangent = gaussian(streams_of[1], (TOKENS, D), 1.0, 6.0, ((0, 32),), jnp.float32)
    segment_ids = draw_segment_ids(jax.random.fold_in(streams_of[40], 71), 0)
    positions = draw_positions(jax.random.fold_in(streams_of[40], 71), 0)
    heads_weight = draw_heads_weight(jax.random.fold_in(streams_of[40], 71), 0)
    heads_weight_first = gaussian(streams_of[5], (D, 3, D), 10.0, 64.0, ((0, 16), (2, 2)), jnp.float32)
    heads_weight_second = jnp.clip(jnp.exp(math.log(2000.0) - 4.6051702 * jax.random.uniform(streams_of[6], (D, 3, D), jnp.float32) ** block_scale(streams_of[6], (D, 3, D), ((0, 16), (2, 2)), -0.2, 0.2)), 20.0, 2000.0)
    output_weight = gaussian(streams_of[7], (D, D), (D // 16) ** -0.5, 0.875, ((0, 32),), jnp.float32)
    output_weight_first = gaussian(streams_of[8], (D, D), 10.0, 64.0, ((0, 32),), jnp.float32)
    output_weight_second = jnp.clip(jnp.exp(math.log(2000.0) - 4.6051702 * jax.random.uniform(streams_of[9], (D, D), jnp.float32) ** block_scale(streams_of[9], (D, D), ((0, 32),), -0.2, 0.2)), 20.0, 2000.0)
    expand_weight = gaussian(streams_of[10], (D, FF), D ** -0.5, 0.21875, ((0, 16), (1, 2)), jnp.float32)
    expand_weight_first = gaussian(streams_of[11], (D, FF), 10.0, 64.0, ((0, 16), (1, 2)), jnp.float32)
    expand_weight_second = jnp.clip(jnp.exp(math.log(2000.0) - 4.6051702 * jax.random.uniform(streams_of[12], (D, FF), jnp.float32) ** block_scale(streams_of[12], (D, FF), ((0, 16), (1, 2)), -0.2, 0.2)), 20.0, 2000.0)
    shrink_weight = gaussian(streams_of[13], (FF, D), FF ** -0.5, 0.109375, ((0, 32),), jnp.float32)
    shrink_weight_first = gaussian(streams_of[14], (FF, D), 10.0, 64.0, ((0, 32),), jnp.float32)
    shrink_weight_second = jnp.clip(jnp.exp(math.log(2000.0) - 4.6051702 * jax.random.uniform(streams_of[15], (FF, D), jnp.float32) ** block_scale(streams_of[15], (FF, D), ((0, 32),), -0.2, 0.2)), 20.0, 2000.0)
    attention_gain = jnp.clip(1.0 + 0.1 * jax.random.normal(streams_of[16], (D,), jnp.float32), 0.5, 1.5)
    attention_gain_first = gaussian(streams_of[17], (D,), 30.0, 192.0, ((0, 32),), jnp.float32)
    attention_gain_second = jnp.clip(jnp.exp(math.log(10000.0) - 4.6051702 * jax.random.uniform(streams_of[18], (D,), jnp.float32) ** block_scale(streams_of[18], (D,), ((0, 32),), -0.2, 0.2)), 100.0, 10000.0)
    attention_shift = gaussian(streams_of[19], (D,), 0.3, 1.75, ((0, 32),), jnp.float32)
    attention_shift_first = gaussian(streams_of[20], (D,), 30.0, 192.0, ((0, 32),), jnp.float32)
    attention_shift_second = jnp.clip(jnp.exp(math.log(10000.0) - 4.6051702 * jax.random.uniform(streams_of[21], (D,), jnp.float32) ** block_scale(streams_of[21], (D,), ((0, 32),), -0.2, 0.2)), 100.0, 10000.0)
    feedforward_gain = jnp.clip(1.0 + 0.1 * jax.random.normal(streams_of[22], (D,), jnp.float32), 0.5, 1.5)
    feedforward_gain_first = gaussian(streams_of[23], (D,), 30.0, 192.0, ((0, 32),), jnp.float32)
    feedforward_gain_second = jnp.clip(jnp.exp(math.log(10000.0) - 4.6051702 * jax.random.uniform(streams_of[24], (D,), jnp.float32) ** block_scale(streams_of[24], (D,), ((0, 32),), -0.2, 0.2)), 100.0, 10000.0)
    feedforward_shift = gaussian(streams_of[25], (D,), 0.3, 1.75, ((0, 32),), jnp.float32)
    feedforward_shift_first = gaussian(streams_of[26], (D,), 30.0, 192.0, ((0, 32),), jnp.float32)
    feedforward_shift_second = jnp.clip(jnp.exp(math.log(10000.0) - 4.6051702 * jax.random.uniform(streams_of[27], (D,), jnp.float32) ** block_scale(streams_of[27], (D,), ((0, 32),), -0.2, 0.2)), 100.0, 10000.0)
    heads_bias = gaussian(streams_of[28], (3 * D,), 0.3, 1.75, ((0, 32),), jnp.float32)
    heads_bias_first = gaussian(streams_of[29], (3 * D,), 30.0, 192.0, ((0, 32),), jnp.float32)
    heads_bias_second = jnp.clip(jnp.exp(math.log(10000.0) - 4.6051702 * jax.random.uniform(streams_of[30], (3 * D,), jnp.float32) ** block_scale(streams_of[30], (3 * D,), ((0, 32),), -0.2, 0.2)), 100.0, 10000.0)
    output_bias = gaussian(streams_of[31], (D,), 0.3, 1.75, ((0, 32),), jnp.float32)
    output_bias_first = gaussian(streams_of[32], (D,), 30.0, 192.0, ((0, 32),), jnp.float32)
    output_bias_second = jnp.clip(jnp.exp(math.log(10000.0) - 4.6051702 * jax.random.uniform(streams_of[33], (D,), jnp.float32) ** block_scale(streams_of[33], (D,), ((0, 32),), -0.2, 0.2)), 100.0, 10000.0)
    expand_bias = gaussian(streams_of[34], (FF,), 0.3, 1.75, ((0, 32),), jnp.float32)
    expand_bias_first = gaussian(streams_of[35], (FF,), 30.0, 192.0, ((0, 32),), jnp.float32)
    expand_bias_second = jnp.clip(jnp.exp(math.log(10000.0) - 4.6051702 * jax.random.uniform(streams_of[36], (FF,), jnp.float32) ** block_scale(streams_of[36], (FF,), ((0, 32),), -0.2, 0.2)), 100.0, 10000.0)
    shrink_bias = gaussian(streams_of[37], (D,), 0.3, 1.75, ((0, 32),), jnp.float32)
    shrink_bias_first = gaussian(streams_of[38], (D,), 30.0, 192.0, ((0, 32),), jnp.float32)
    shrink_bias_second = jnp.clip(jnp.exp(math.log(10000.0) - 4.6051702 * jax.random.uniform(streams_of[39], (D,), jnp.float32) ** block_scale(streams_of[39], (D,), ((0, 32),), -0.2, 0.2)), 100.0, 10000.0)
    return dict(block_input=block_input, cotangent=cotangent, segment_ids=segment_ids, positions=positions, heads_weight=heads_weight, heads_weight_first=heads_weight_first, heads_weight_second=heads_weight_second, output_weight=output_weight, output_weight_first=output_weight_first, output_weight_second=output_weight_second, expand_weight=expand_weight, expand_weight_first=expand_weight_first, expand_weight_second=expand_weight_second, shrink_weight=shrink_weight, shrink_weight_first=shrink_weight_first, shrink_weight_second=shrink_weight_second, attention_gain=attention_gain, attention_gain_first=attention_gain_first, attention_gain_second=attention_gain_second, attention_shift=attention_shift, attention_shift_first=attention_shift_first, attention_shift_second=attention_shift_second, feedforward_gain=feedforward_gain, feedforward_gain_first=feedforward_gain_first, feedforward_gain_second=feedforward_gain_second, feedforward_shift=feedforward_shift, feedforward_shift_first=feedforward_shift_first, feedforward_shift_second=feedforward_shift_second, heads_bias=heads_bias, heads_bias_first=heads_bias_first, heads_bias_second=heads_bias_second, output_bias=output_bias, output_bias_first=output_bias_first, output_bias_second=output_bias_second, expand_bias=expand_bias, expand_bias_first=expand_bias_first, expand_bias_second=expand_bias_second, shrink_bias=shrink_bias, shrink_bias_first=shrink_bias_first, shrink_bias_second=shrink_bias_second)


EPS_NORM = 1e-05
LEARN_RATE = 0.006
BETA_ONE = 0.9
BETA_TWO = 0.95
EPS_ADAM = 1e-08
DECAY = 0.01
NEG_LARGE = -1e+30
ROOT_HALF = 0.7071067811865476
ROOT_TWO_PI = 2.5066282746310002

def gelu_value(values):
    return 0.5 * values * (1.0 + jax.scipy.special.erf(values * ROOT_HALF))

def gelu_slope(values):
    return 0.5 * (1.0 + jax.scipy.special.erf(values * ROOT_HALF)) + values * jnp.exp(-0.5 * values * values) / ROOT_TWO_PI

def rotary_tables(offsets):
    ladder = jnp.arange(RD // 2, dtype=jnp.float32)
    frequency = jnp.power(10000.0, -2.0 * ladder / RD)
    angles = offsets.astype(jnp.float32)[:, None] * frequency[None, :]
    cosine = jnp.concatenate([jnp.cos(angles), jnp.cos(angles)], axis=1)[:, None, :]
    sine = jnp.concatenate([jnp.sin(angles), jnp.sin(angles)], axis=1)[:, None, :]
    return (cosine, sine)

def rotary_apply(values, cosine, sine):
    half = RD // 2
    turning = values[..., :RD]
    swapped = jnp.concatenate([-turning[..., half:], turning[..., :half]], axis=-1)
    return jnp.concatenate([turning * cosine + swapped * sine, values[..., RD:]], axis=-1)

def rotary_back(grads, cosine, sine):
    half = RD // 2
    turning = grads[..., :RD]
    scaled = turning * sine
    swapped = jnp.concatenate([scaled[..., half:], -scaled[..., :half]], axis=-1)
    return jnp.concatenate([turning * cosine + swapped, grads[..., RD:]], axis=-1)

def head_forward(query, keyed, valued, allowed):
    scores = jnp.where(allowed, jnp.dot(query, keyed.T, preferred_element_type=jnp.float32) * HD ** (-0.5), NEG_LARGE)
    peak = lax.optimization_barrier(jnp.max(scores, axis=1, keepdims=True))
    total = peak + jnp.log(lax.optimization_barrier(jnp.sum(jnp.exp(scores - peak), axis=1, keepdims=True)))
    weights_low = jnp.exp(scores - total).astype(jnp.bfloat16)
    return (jnp.dot(weights_low, valued, preferred_element_type=jnp.float32), total)

def head_backward(query, keyed, valued, context_grad, total, allowed):
    scale = HD ** (-0.5)
    scores = jnp.where(allowed, jnp.dot(query, keyed.T, preferred_element_type=jnp.float32) * scale, NEG_LARGE)
    probs = jnp.exp(scores - total)
    weights_low = probs.astype(jnp.bfloat16)
    prob_grad = jnp.dot(context_grad, valued.T, preferred_element_type=jnp.float32)
    delta = lax.optimization_barrier(jnp.sum(probs * prob_grad, axis=1, keepdims=True))
    score_grad = (probs * (prob_grad - delta) * scale).astype(jnp.bfloat16)
    query_grad = jnp.dot(score_grad, keyed, preferred_element_type=jnp.float32)
    key_grad = jnp.dot(score_grad.T, query, preferred_element_type=jnp.float32)
    value_grad = jnp.dot(weights_low.T, context_grad, preferred_element_type=jnp.float32)
    return (query_grad, key_grad, value_grad)

def pack_pass(matrices, vectors, inputs, upstream, segments, offsets):
    heads_low, output_low, expand_low, shrink_low = matrices
    gain_one, shift_one, gain_two, shift_two, heads_bias, output_bias, expand_bias, shrink_bias = vectors
    rows = inputs.shape[0]
    width = inputs.shape[1]
    heads = width // HD
    centred = inputs - lax.optimization_barrier(jnp.mean(inputs, axis=1, keepdims=True))
    inverse = lax.rsqrt(lax.optimization_barrier(jnp.mean(centred * centred, axis=1, keepdims=True)) + EPS_NORM)
    normalised = centred * inverse
    attend_input = (normalised * gain_one + shift_one).astype(jnp.bfloat16)
    feed_input = (normalised * gain_two + shift_two).astype(jnp.bfloat16)
    mixed = jnp.dot(attend_input, heads_low.reshape(width, 3 * width), preferred_element_type=jnp.float32).reshape(rows, 3, width) + heads_bias.reshape(3, width)
    cosine, sine = rotary_tables(offsets)
    queries = jnp.transpose(rotary_apply(mixed[:, 0].reshape(rows, heads, HD), cosine, sine), (1, 0, 2)).astype(jnp.bfloat16)
    keys = jnp.transpose(rotary_apply(mixed[:, 1].reshape(rows, heads, HD), cosine, sine), (1, 0, 2)).astype(jnp.bfloat16)
    values = jnp.transpose(mixed[:, 2].reshape(rows, heads, HD), (1, 0, 2)).astype(jnp.bfloat16)
    places = jnp.arange(rows, dtype=jnp.int32)
    allowed = (segments[:, None] == segments[None, :]) & (places[:, None] >= places[None, :])

    def forward_head(operands):
        return head_forward(operands[0], operands[1], operands[2], allowed)
    context, totals = lax.map(forward_head, (queries, keys, values))
    context_low = jnp.transpose(context, (1, 0, 2)).reshape(rows, width).astype(jnp.bfloat16)
    expanded = jnp.dot(feed_input, expand_low, preferred_element_type=jnp.float32) + expand_bias
    activated = gelu_value(expanded).astype(jnp.bfloat16)
    branches = jnp.dot(context_low, output_low, preferred_element_type=jnp.float32) + jnp.dot(activated, shrink_low, preferred_element_type=jnp.float32)
    block_output = inputs + branches + output_bias + shrink_bias
    upstream_low = upstream.astype(jnp.bfloat16)
    upstream_sum = lax.optimization_barrier(jnp.sum(upstream, axis=0))
    output_grad = jnp.dot(context_low.T, upstream_low, preferred_element_type=jnp.float32)
    shrink_grad = jnp.dot(activated.T, upstream_low, preferred_element_type=jnp.float32)
    context_grad = jnp.dot(upstream_low, output_low.T, preferred_element_type=jnp.float32).astype(jnp.bfloat16)
    context_heads = jnp.transpose(context_grad.reshape(rows, heads, HD), (1, 0, 2))
    expanded_grad = jnp.dot(upstream_low, shrink_low.T, preferred_element_type=jnp.float32) * gelu_slope(expanded)
    expand_bias_grad = lax.optimization_barrier(jnp.sum(expanded_grad, axis=0))
    expanded_low = expanded_grad.astype(jnp.bfloat16)
    expand_grad = jnp.dot(feed_input.T, expanded_low, preferred_element_type=jnp.float32)
    feed_grad = jnp.dot(expanded_low, expand_low.T, preferred_element_type=jnp.float32)

    def backward_head(operands):
        return head_backward(operands[0], operands[1], operands[2], operands[3], operands[4], allowed)
    query_grad, key_grad, value_grad = lax.map(backward_head, (queries, keys, values, context_heads, totals))
    query_grad = rotary_back(jnp.transpose(query_grad, (1, 0, 2)), cosine, sine)
    key_grad = rotary_back(jnp.transpose(key_grad, (1, 0, 2)), cosine, sine)
    value_grad = jnp.transpose(value_grad, (1, 0, 2))
    mixed_grad = jnp.stack([query_grad.reshape(rows, width), key_grad.reshape(rows, width), value_grad.reshape(rows, width)], axis=1)
    heads_bias_grad = lax.optimization_barrier(jnp.sum(mixed_grad, axis=0)).reshape(3 * width)
    mixed_low = mixed_grad.reshape(rows, 3 * width).astype(jnp.bfloat16)
    heads_grad = jnp.dot(attend_input.T, mixed_low, preferred_element_type=jnp.float32).reshape(width, 3, width)
    attend_grad = jnp.dot(mixed_low, heads_low.reshape(width, 3 * width).T, preferred_element_type=jnp.float32)
    gain_one_grad = lax.optimization_barrier(jnp.sum(attend_grad * normalised, axis=0))
    shift_one_grad = lax.optimization_barrier(jnp.sum(attend_grad, axis=0))
    gain_two_grad = lax.optimization_barrier(jnp.sum(feed_grad * normalised, axis=0))
    shift_two_grad = lax.optimization_barrier(jnp.sum(feed_grad, axis=0))
    direct = attend_grad * gain_one + feed_grad * gain_two
    input_grad = upstream + inverse * (direct - lax.optimization_barrier(jnp.mean(direct, axis=1, keepdims=True)) - normalised * lax.optimization_barrier(jnp.mean(direct * normalised, axis=1, keepdims=True)))
    gradients = (heads_grad, output_grad, expand_grad, shrink_grad, gain_one_grad, shift_one_grad, gain_two_grad, shift_two_grad, heads_bias_grad, upstream_sum, expand_bias_grad, upstream_sum)
    return (block_output, input_grad, gradients)

def adamw(param, first, second, gradient, decay):
    first_next = BETA_ONE * first + (1.0 - BETA_ONE) * gradient
    second_next = BETA_TWO * second + (1.0 - BETA_TWO) * gradient * gradient
    moment = first_next / (1.0 - BETA_ONE ** ADAM_STEP)
    square = second_next / (1.0 - BETA_TWO ** ADAM_STEP)
    param_next = param - LEARN_RATE * (moment / (jnp.sqrt(square) + EPS_ADAM) + decay * param)
    return (param_next, first_next, second_next)

def reference(block_input, cotangent, segment_ids, positions, heads_weight, heads_weight_first, heads_weight_second, output_weight, output_weight_first, output_weight_second, expand_weight, expand_weight_first, expand_weight_second, shrink_weight, shrink_weight_first, shrink_weight_second, attention_gain, attention_gain_first, attention_gain_second, attention_shift, attention_shift_first, attention_shift_second, feedforward_gain, feedforward_gain_first, feedforward_gain_second, feedforward_shift, feedforward_shift_first, feedforward_shift_second, heads_bias, heads_bias_first, heads_bias_second, output_bias, output_bias_first, output_bias_second, expand_bias, expand_bias_first, expand_bias_second, shrink_bias, shrink_bias_first, shrink_bias_second):
    params = (heads_weight, output_weight, expand_weight, shrink_weight, attention_gain, attention_shift, feedforward_gain, feedforward_shift, heads_bias, output_bias, expand_bias, shrink_bias)
    firsts = (heads_weight_first, output_weight_first, expand_weight_first, shrink_weight_first, attention_gain_first, attention_shift_first, feedforward_gain_first, feedforward_shift_first, heads_bias_first, output_bias_first, expand_bias_first, shrink_bias_first)
    seconds = (heads_weight_second, output_weight_second, expand_weight_second, shrink_weight_second, attention_gain_second, attention_shift_second, feedforward_gain_second, feedforward_shift_second, heads_bias_second, output_bias_second, expand_bias_second, shrink_bias_second)
    matrices = tuple((weight.astype(jnp.bfloat16) for weight in params[:4]))
    vectors = params[4:]
    packs = block_input.shape[0] // TOK_DEV
    width = block_input.shape[1]

    def scan_step(carry, items):
        inputs, upstream, segments, offsets = items
        output_rows, input_rows, gradients = pack_pass(matrices, vectors, inputs, upstream, segments, offsets)
        return (tuple((running + piece for running, piece in zip(carry, gradients))), (output_rows, input_rows))
    start = tuple((jnp.zeros(weight.shape, jnp.float32) for weight in params))
    gradients, (outputs, input_rows) = lax.scan(scan_step, start, (block_input.reshape(packs, TOK_DEV, width), cotangent.reshape(packs, TOK_DEV, width), segment_ids.reshape(packs, TOK_DEV), positions.reshape(packs, TOK_DEV)))
    results = [outputs.reshape(packs * TOK_DEV, width), input_rows.reshape(packs * TOK_DEV, width)]
    for number in range(12):
        decay = DECAY if number < 4 else 0.0
        param_next, first_next, second_next = adamw(params[number], firsts[number], seconds[number], gradients[number], decay)
        results.extend([gradients[number], param_next, first_next, second_next])
    return tuple(results)
```

```python
import functools

import jax
import jax.numpy as jnp
from jax import lax
from jax.experimental import pallas as pl
from jax.experimental.pallas import tpu as pltpu
from jax.sharding import PartitionSpec as P


HD = 64
RD = 16
ADAM_STEP = 3


EPS_NORM = 1e-05
LEARN_RATE = 0.006
BETA_ONE = 0.9
BETA_TWO = 0.95
EPS_ADAM = 1e-08
DECAY = 0.01
NEG_LARGE = -1e30
ROOT_HALF = 0.7071067811865476
ROOT_TWO_PI = 2.5066282746310002


LANES = 128


def gelu_value(values):
    return 0.5 * values * (1.0 + jax.scipy.special.erf(values * ROOT_HALF))


def gelu_slope(values):
    return (
        0.5 * (1.0 + jax.scipy.special.erf(values * ROOT_HALF))
        + values * jnp.exp(-0.5 * values * values) / ROOT_TWO_PI
    )


def layer_statistics(inputs):
    centred = inputs - jnp.mean(inputs, axis=1, keepdims=True)
    inverse = lax.rsqrt(jnp.mean(centred * centred, axis=1, keepdims=True) + EPS_NORM)
    return (centred * inverse, inverse)


def adamw(param, first, second, gradient, decay):
    first_next = BETA_ONE * first + (1.0 - BETA_ONE) * gradient
    second_next = BETA_TWO * second + (1.0 - BETA_TWO) * gradient * gradient
    moment = first_next / (1.0 - BETA_ONE**ADAM_STEP)
    square = second_next / (1.0 - BETA_TWO**ADAM_STEP)
    param_next = param - LEARN_RATE * (moment / (jnp.sqrt(square) + EPS_ADAM) + decay * param)
    return (param_next, first_next, second_next)


def dp_bits():
    return (lax.axis_size("dp") - 1).bit_length()


def swap(value, bit):
    count = lax.axis_size("dp")
    return lax.ppermute(value, "dp", [(place, place ^ (1 << bit)) for place in range(count)])


def pair_swap(value):
    return lax.ppermute(value, "tensor", [(0, 1), (1, 0)])


def sides(bit):
    return ((lax.axis_index("dp") >> bit) & 1) == 1


def cross(value, first, second):
    count = lax.axis_size("dp")
    flips = (1 << first, 1 << second)
    moves = [
        (2 * place + rank, 2 * (place ^ flips[rank]) + rank)
        for place in range(count)
        for rank in range(2)
    ]
    return lax.ppermute(value, ("dp", "tensor"), moves)


def pick(whole, place, axis):
    return lax.dynamic_index_in_dim(whole, place.astype(jnp.int32), axis, keepdims=False)


def total_of(keep, other, kind):
    return (keep.astype(jnp.float32) + other.astype(jnp.float32)).astype(kind)


def low_gather(own, axis):
    even = lax.axis_index("tensor") == 0
    right, down = sides(0), sides(1)
    near = cross(own, 1, 0)
    far = cross(jnp.stack([own, near]), 0, 1)
    below = jnp.where(even, near, far[0])
    beside = jnp.where(even, far[0], near)
    top = (jnp.where(right, beside, own), jnp.where(right, own, beside))
    base = (jnp.where(right, far[1], below), jnp.where(right, below, far[1]))
    upper = jnp.stack([jnp.where(down, b, t) for t, b in zip(top, base)], axis=axis)
    lower = jnp.stack([jnp.where(down, t, b) for t, b in zip(top, base)], axis=axis)
    return jnp.stack([upper, lower], axis=axis)


def low_scatter(whole, axis, kind):
    even = lax.axis_index("tensor") == 0
    right, down = sides(0), sides(1)
    keep = jnp.where(even, pick(whole, right, axis + 1), pick(whole, down, axis))
    send = jnp.where(even, pick(whole, ~right, axis + 1), pick(whole, ~down, axis))
    half = total_of(keep, cross(send, 0, 1), whole.dtype)
    place = jnp.where(even, down, right)
    other = cross(pick(half, ~place, axis), 1, 0)
    return total_of(pick(half, place, axis), other, kind)


def gather_rows(piece, low_first=False):
    uppers = list(range(dp_bits() - 1, 1, -1))
    current = low_gather(piece, 0) if low_first else piece
    for count, bit in enumerate(uppers):
        other = swap(current, bit)
        upper = sides(bit)
        current = jnp.stack(
            [jnp.where(upper, other, current), jnp.where(upper, current, other)], axis=count
        )
    if not low_first:
        current = low_gather(current, len(uppers))
    return current.reshape((-1,) + piece.shape)


def scatter_rows(whole, low_first=True):
    bits = dp_bits()
    shape = whole.shape[1:]
    current = whole.reshape((2,) * bits + shape)
    if low_first:
        current = low_scatter(current, bits - 2, whole.dtype)
    for bit in range(2, bits):
        place = sides(bit)
        axis = bits - 1 - bit
        last = low_first and bit == bits - 1
        kind = jnp.float32 if last else whole.dtype
        other = swap(pick(current, ~place, axis), bit)
        current = total_of(pick(current, place, axis), other, kind)
    if not low_first:
        current = low_scatter(current, 0, jnp.float32)
    return current


def pair_gather(piece):
    other = pair_swap(piece)
    upper = lax.axis_index("tensor") == 1
    return jnp.concatenate(
        [jnp.where(upper, other, piece), jnp.where(upper, piece, other)], axis=0
    )


def pair_scatter(whole):
    half = whole.shape[0] // 2
    rank = lax.axis_index("tensor")
    keep = lax.dynamic_slice_in_dim(whole, rank * half, half, 0)
    send = lax.dynamic_slice_in_dim(whole, (1 - rank) * half, half, 0)
    return keep + pair_swap(send.astype(jnp.bfloat16)).astype(jnp.float32)


def gather_vectors(vectors):
    packed = jnp.concatenate(vectors)[None]
    packed = pair_gather(packed)
    whole = gather_rows(packed).reshape(-1, packed.shape[1])
    results, offset = [], 0
    for vector in vectors:
        size = vector.shape[0]
        results.append(whole[:, offset : offset + size].reshape(-1))
        offset += size
    return results


def scatter_vectors(wholes):
    devices = lax.axis_size("dp") * 2
    packed = jnp.concatenate([whole.reshape(devices, -1) for whole in wholes], axis=1)
    columns = packed.shape[1]
    own = scatter_rows(packed.reshape(devices // 2, 2, columns))
    rank = lax.axis_index("tensor")
    own = pick(own, rank, 0) + pair_swap(pick(own, 1 - rank, 0))
    results, offset = [], 0
    for whole in wholes:
        size = whole.size // devices
        results.append(own[offset : offset + size])
        offset += size
    return tuple(results)


def lane_tables(offsets):
    half = RD // 2
    lanes = jnp.arange(LANES, dtype=jnp.int32) % HD
    frequency = jnp.power(10000.0, -2.0 * (lanes % half).astype(jnp.float32) / RD)
    angles = offsets.astype(jnp.float32)[:, None] * frequency[None, :]
    turned = (lanes < RD)[None, :]
    cosine = jnp.where(turned, jnp.cos(angles), 1.0)
    sine = jnp.sin(angles)
    ahead = jnp.where((lanes < half)[None, :], -sine, 0.0)
    behind = jnp.where((lanes >= half)[None, :] & turned, sine, 0.0)
    return (cosine, ahead, behind)


def product(left, right, left_axis, right_axis):
    return lax.dot_general(
        left,
        right,
        (((left_axis,), (right_axis,)), ((), ())),
        preferred_element_type=jnp.float32,
    )


def attention_kernel(
    pair,
    attend_ref,
    upstream_ref,
    heads_ref,
    output_ref,
    bias_ref,
    cosine_ref,
    ahead_ref,
    behind_ref,
    segment_column_ref,
    segment_row_ref,
    branch_in_ref,
    attend_in_ref,
    heads_grad_ref,
    output_grad_ref,
    bias_grad_ref,
    branch_ref,
    attend_grad_ref,
    key_grad_ref,
    value_grad_ref,
):
    low = jnp.bfloat16
    rows = attend_ref.shape[0]
    local_width = heads_ref.shape[1] // 3
    scale = HD ** (-0.5)
    attend, upstream = attend_ref[...], upstream_ref[...]
    cosine, ahead, behind = cosine_ref[...], ahead_ref[...], behind_ref[...]
    starts = [which * local_width + pair * LANES for which in range(3)]

    def project(which):
        columns = slice(starts[which], starts[which] + LANES)
        return product(attend, heads_ref[:, columns], 1, 0) + bias_ref[:, columns]

    def turn(value, sign):
        forward = pltpu.roll(value, LANES - RD // 2, 1) * ahead
        return value * cosine + sign * (forward + pltpu.roll(value, RD // 2, 1) * behind)

    query = (turn(project(0), 1.0).astype(low).astype(jnp.float32) * scale).astype(low)
    key = turn(project(1), 1.0).astype(low)
    value = project(2).astype(low)
    output_rows = output_ref[pair * LANES : (pair + 1) * LANES, :]
    context_grad = product(upstream, output_rows, 1, 1).astype(low)

    key_grad_ref[...] = jnp.zeros_like(key_grad_ref)
    value_grad_ref[...] = jnp.zeros_like(value_grad_ref)
    block = rows // 2
    contexts, query_grads = [], []
    for step in range(2):
        span = slice(step * block, (step + 1) * block)
        reach = (step + 1) * block
        same = segment_column_ref[span, :] == segment_row_ref[:, :reach]
        place = lax.broadcasted_iota(jnp.int32, (block, reach), 0) + step * block
        allowed = same & (place >= lax.broadcasted_iota(jnp.int32, (block, reach), 1))
        lanes = lax.broadcasted_iota(jnp.int32, (block, LANES), 1)

        def one_head(head, carried, span=span, reach=reach, allowed=allowed, lanes=lanes):
            context, query_grad = carried
            mine = (lanes >= head * HD) & (lanes < (head + 1) * HD)
            own_query = jnp.where(mine, query[span].astype(jnp.float32), 0.0).astype(low)
            own_grad = jnp.where(mine, context_grad[span].astype(jnp.float32), 0.0).astype(low)
            scores = jnp.where(allowed, product(own_query, key[:reach], 1, 1), NEG_LARGE)
            peak = jnp.max(scores, axis=1, keepdims=True)
            raised = jnp.exp(scores - peak)
            probs = raised * (1.0 / jnp.sum(raised, axis=1, keepdims=True))
            weights_low = probs.astype(low)
            context = jnp.where(mine, product(weights_low, value[:reach], 1, 0), context)
            prob_grad = product(own_grad, value[:reach], 1, 1)
            delta = jnp.sum(probs * prob_grad, axis=1, keepdims=True)
            score_grad = (probs * (prob_grad - delta)).astype(low)
            query_grad = jnp.where(mine, product(score_grad, key[:reach], 1, 0), query_grad)
            key_grad_ref[:reach, :] += product(score_grad, own_query, 0, 0)
            value_grad_ref[:reach, :] += product(weights_low, own_grad, 0, 0)
            return (context, query_grad)

        blank = jnp.zeros((block, LANES), jnp.float32)
        context, query_grad = lax.fori_loop(0, LANES // HD, one_head, (blank, blank))
        contexts.append(context.astype(low))
        query_grads.append(query_grad * scale)
    context_low = jnp.concatenate(contexts, axis=0)
    output_grad_ref[...] = product(context_low, upstream, 0, 0).astype(low)
    branch_ref[...] = branch_in_ref[...] + product(context_low, output_rows, 1, 0)
    attend_grad = attend_in_ref[...]
    grads = (
        turn(jnp.concatenate(query_grads, axis=0), -1.0),
        turn(key_grad_ref[...], -1.0),
        value_grad_ref[...],
    )
    for which, grad in enumerate(grads):
        columns = slice(which * LANES, (which + 1) * LANES)
        bias_grad_ref[:, columns] = jnp.sum(grad, axis=0, keepdims=True)
        grad_low = grad.astype(low)
        heads_grad_ref[:, columns] = product(attend, grad_low, 0, 0).astype(low)
        weight = heads_ref[:, starts[which] : starts[which] + LANES]
        attend_grad = attend_grad + product(grad_low, weight, 1, 1)
    attend_grad_ref[...] = attend_grad


def attention_pair(pair, operands, branch, attend_grad):
    attend = operands[0]
    rows, width = attend.shape
    low = jnp.bfloat16
    shapes = (
        ((width, 3 * LANES), low),
        ((LANES, width), low),
        ((1, 3 * LANES), jnp.float32),
        ((rows, width), jnp.float32),
        ((rows, width), jnp.float32),
    )
    space = pl.BlockSpec(memory_space=pltpu.VMEM)
    count = len(operands)
    return pl.pallas_call(
        functools.partial(attention_kernel, pair),
        out_shape=[jax.ShapeDtypeStruct(*each) for each in shapes],
        in_specs=[space] * (count + 2),
        out_specs=[space] * len(shapes),
        scratch_shapes=[pltpu.VMEM((rows, LANES), jnp.float32)] * 2,
        input_output_aliases={count: 3, count + 1: 4},
        compiler_params=pltpu.CompilerParams(vmem_limit_bytes=12 * 1024 * 1024),
        cost_estimate=pl.CostEstimate(
            flops=6 * rows * width * LANES * 8, transcendentals=0, bytes_accessed=8 << 20
        ),
    )(*operands, branch, attend_grad)


def on_device(
    block_input,
    cotangent,
    segment_ids,
    positions,
    heads_weight,
    heads_weight_first,
    heads_weight_second,
    output_weight,
    output_weight_first,
    output_weight_second,
    expand_weight,
    expand_weight_first,
    expand_weight_second,
    shrink_weight,
    shrink_weight_first,
    shrink_weight_second,
    attention_gain,
    attention_gain_first,
    attention_gain_second,
    attention_shift,
    attention_shift_first,
    attention_shift_second,
    feedforward_gain,
    feedforward_gain_first,
    feedforward_gain_second,
    feedforward_shift,
    feedforward_shift_first,
    feedforward_shift_second,
    heads_bias,
    heads_bias_first,
    heads_bias_second,
    output_bias,
    output_bias_first,
    output_bias_second,
    expand_bias,
    expand_bias_first,
    expand_bias_second,
    shrink_bias,
    shrink_bias_first,
    shrink_bias_second,
):
    tensor_rank = lax.axis_index("tensor")
    width = block_input.shape[1]
    local_width = heads_weight.shape[2]
    local_hidden = expand_weight.shape[1]
    low = jnp.bfloat16

    input_all = pair_gather(block_input)
    upstream_all = pair_gather(cotangent.astype(low))
    vectors = (
        attention_gain,
        attention_shift,
        feedforward_gain,
        feedforward_shift,
        heads_bias,
        output_bias,
        expand_bias,
        shrink_bias,
    )
    (
        gain_one,
        shift_one,
        gain_two,
        shift_two,
        heads_bias_all,
        output_bias_all,
        expand_bias_all,
        shrink_bias_all,
    ) = gather_vectors(vectors)
    expand_low = gather_rows(expand_weight.astype(low)).reshape(width, local_hidden)
    shrink_low = gather_rows(shrink_weight.astype(low)).reshape(local_hidden, width)
    heads_flat = heads_weight.astype(low).reshape(-1, 3 * local_width)
    short, tall = output_weight.shape[0], heads_flat.shape[0]
    packed = gather_rows(
        jnp.concatenate(
            [
                output_weight.astype(low),
                heads_flat[:, :width],
                jnp.concatenate([heads_flat[:short, width:], heads_flat[short:, width:]], axis=1),
            ],
            axis=0,
        ),
        low_first=True,
    )
    output_low = packed[:, :short].reshape(local_width, width)
    thirds = packed[:, short + tall :]
    thirds = jnp.concatenate([thirds[..., :local_width], thirds[..., local_width:]], axis=1)
    heads_low = jnp.concatenate([packed[:, short : short + tall], thirds], axis=2)
    heads_low = heads_low.reshape(width, 3 * local_width)

    heads_bias_local = lax.dynamic_slice_in_dim(
        heads_bias_all.reshape(3, width), tensor_rank * local_width, local_width, 1
    )
    expand_bias_local = lax.dynamic_slice_in_dim(
        expand_bias_all, tensor_rank * local_hidden, local_hidden, 0
    )
    normalised, inverse = layer_statistics(block_input)
    normalised_all, _ = layer_statistics(input_all)
    attend_input = (normalised_all * gain_one + shift_one).astype(low)
    feed_input = (normalised_all * gain_two + shift_two).astype(low)
    rows = attend_input.shape[0]

    expanded = (
        jnp.dot(feed_input, expand_low, preferred_element_type=jnp.float32) + expand_bias_local
    )
    activated = gelu_value(expanded).astype(low)
    shrink_grad = jnp.dot(activated.T, upstream_all, preferred_element_type=jnp.float32)
    shrink_own = scatter_rows(shrink_grad.astype(low).reshape((-1,) + shrink_weight.shape))
    expanded_grad = jnp.dot(
        upstream_all, shrink_low.T, preferred_element_type=jnp.float32
    ) * gelu_slope(expanded)
    expanded_low = expanded_grad.astype(low)
    expand_grad = jnp.dot(feed_input.T, expanded_low, preferred_element_type=jnp.float32)
    expand_own = scatter_rows(expand_grad.astype(low).reshape((-1,) + expand_weight.shape))
    feed_grad = jnp.dot(expanded_low, expand_low.T, preferred_element_type=jnp.float32)
    feed_own = pair_scatter(feed_grad)

    branch = jnp.dot(activated, shrink_low, preferred_element_type=jnp.float32)
    attend_grad = jnp.zeros((rows, width), jnp.float32)
    operands = (
        attend_input,
        upstream_all,
        heads_low,
        output_low,
        heads_bias_local.reshape(1, 3 * local_width),
        *lane_tables(positions),
        segment_ids[:, None],
        segment_ids[None, :],
    )
    heads_grads, output_grads, bias_grads = [], [], []
    for pair in range(local_width // LANES):
        heads_grad, output_grad, bias_grad, branch, attend_grad = attention_pair(
            pair, operands, branch, attend_grad
        )
        heads_grads.append(heads_grad)
        output_grads.append(output_grad)
        bias_grads.append(bias_grad.reshape(3, LANES))
    heads_bias_sum = jnp.concatenate(bias_grads, axis=1)
    attend_own = pair_scatter(attend_grad)
    block_output = block_input + pair_scatter(branch) + output_bias_all + shrink_bias_all
    parts = [
        jnp.concatenate(
            [each[:, which * LANES : (which + 1) * LANES] for each in heads_grads], axis=1
        ).reshape(-1, tall, local_width)
        for which in range(3)
    ]
    packed = scatter_rows(
        jnp.concatenate(
            [
                jnp.concatenate(output_grads, axis=0).reshape(-1, short, width),
                jnp.concatenate(parts[:2], axis=2),
                jnp.concatenate([parts[2][:, :short], parts[2][:, short:]], axis=2),
            ],
            axis=1,
        ),
    )
    output_own = packed[:short]
    thirds = packed[short + tall :]
    thirds = jnp.concatenate([thirds[:, :local_width], thirds[:, local_width:]], axis=0)
    heads_own = jnp.concatenate([packed[short : short + tall], thirds], axis=1)
    heads_own = heads_own.reshape(heads_weight.shape)

    gain_sums = (
        jnp.sum(attend_own * normalised, axis=0),
        jnp.sum(attend_own, axis=0),
        jnp.sum(feed_own * normalised, axis=0),
        jnp.sum(feed_own, axis=0),
    )
    direct = attend_own * gain_one + feed_own * gain_two
    input_gradient = cotangent + inverse * (
        direct
        - jnp.mean(direct, axis=1, keepdims=True)
        - normalised * jnp.mean(direct * normalised, axis=1, keepdims=True)
    )
    heads_bias_part = lax.dynamic_update_slice_in_dim(
        jnp.zeros((3, width), jnp.float32), heads_bias_sum, tensor_rank * local_width, 1
    ).reshape(3 * width)
    expand_bias_part = lax.dynamic_update_slice_in_dim(
        jnp.zeros((expand_bias_all.shape[0],), jnp.float32),
        jnp.sum(expanded_grad, axis=0),
        tensor_rank * local_hidden,
        0,
    )
    upstream_sum = jnp.sum(cotangent, axis=0)
    matrix_grads = (heads_own, output_own, expand_own, shrink_own)
    vector_grads = scatter_vectors(
        gain_sums + (heads_bias_part, upstream_sum, expand_bias_part, upstream_sum)
    )
    params = (
        heads_weight,
        output_weight,
        expand_weight,
        shrink_weight,
        attention_gain,
        attention_shift,
        feedforward_gain,
        feedforward_shift,
        heads_bias,
        output_bias,
        expand_bias,
        shrink_bias,
    )
    firsts = (
        heads_weight_first,
        output_weight_first,
        expand_weight_first,
        shrink_weight_first,
        attention_gain_first,
        attention_shift_first,
        feedforward_gain_first,
        feedforward_shift_first,
        heads_bias_first,
        output_bias_first,
        expand_bias_first,
        shrink_bias_first,
    )
    seconds = (
        heads_weight_second,
        output_weight_second,
        expand_weight_second,
        shrink_weight_second,
        attention_gain_second,
        attention_shift_second,
        feedforward_gain_second,
        feedforward_shift_second,
        heads_bias_second,
        output_bias_second,
        expand_bias_second,
        shrink_bias_second,
    )
    gradients = tuple(matrix_grads) + tuple(vector_grads)
    results = [block_output, input_gradient]
    for number in range(12):
        params, firsts, seconds, gradients = (
            each[:number] + (value,) + each[number + 1 :]
            for each, value in zip(
                (params, firsts, seconds, gradients),
                lax.optimization_barrier(
                    (params[number], firsts[number], seconds[number], gradients[number])
                ),
            )
        )
        decay = DECAY if number < 4 else 0.0
        param_next, first_next, second_next = adamw(
            params[number], firsts[number], seconds[number], gradients[number], decay
        )
        results.extend([gradients[number], param_next, first_next, second_next])
    return tuple(results)


def solution(mesh):
    both = ("dp", "tensor")
    tokens, shards = P(both, None), P(both)
    heads, expands = P("dp", None, "tensor"), P("dp", "tensor")
    stacked = P(("tensor", "dp"), None)
    matrices = (heads, stacked, expands, stacked)
    in_specs = (tokens, tokens, P("dp"), P("dp"))
    in_specs += tuple(spec for spec in matrices for _ in range(3)) + (shards,) * 24
    out_specs = (tokens, tokens)
    out_specs += tuple(spec for spec in matrices for _ in range(4)) + (shards,) * 32
    return jax.shard_map(
        on_device, mesh=mesh, in_specs=in_specs, out_specs=out_specs, check_vma=False
    )
```

```python
import jax
import jax.numpy as jnp
from jax import lax
from jax.experimental import pallas as pl
from jax.experimental.pallas import tpu as pltpu
from jax.sharding import PartitionSpec as P


HD = 64
RD = 16
ADAM_STEP = 3


EPS_NORM = 1e-05
LEARN_RATE = 0.006
BETA_ONE = 0.9
BETA_TWO = 0.95
EPS_ADAM = 1e-08
DECAY = 0.01
NEG_LARGE = -1e30
ROOT_HALF = 0.7071067811865476
ROOT_TWO_PI = 2.5066282746310002


LANES = 128


def gelu_value(values):
    return 0.5 * values * (1.0 + jax.scipy.special.erf(values * ROOT_HALF))


def gelu_slope(values):
    return (
        0.5 * (1.0 + jax.scipy.special.erf(values * ROOT_HALF))
        + values * jnp.exp(-0.5 * values * values) / ROOT_TWO_PI
    )


def layer_statistics(inputs):
    centred = inputs - jnp.mean(inputs, axis=1, keepdims=True)
    inverse = lax.rsqrt(jnp.mean(centred * centred, axis=1, keepdims=True) + EPS_NORM)
    return (centred * inverse, inverse)


def adamw(param, first, second, gradient, decay):
    first_next = BETA_ONE * first + (1.0 - BETA_ONE) * gradient
    second_next = BETA_TWO * second + (1.0 - BETA_TWO) * gradient * gradient
    moment = first_next / (1.0 - BETA_ONE**ADAM_STEP)
    square = second_next / (1.0 - BETA_TWO**ADAM_STEP)
    param_next = param - LEARN_RATE * (moment / (jnp.sqrt(square) + EPS_ADAM) + decay * param)
    return (param_next, first_next, second_next)


def dp_bits():
    return (lax.axis_size("dp") - 1).bit_length()


def swap(value, bit):
    count = lax.axis_size("dp")
    return lax.ppermute(value, "dp", [(place, place ^ (1 << bit)) for place in range(count)])


def pair_swap(value):
    return lax.ppermute(value, "tensor", [(0, 1), (1, 0)])


def sides(bit):
    return ((lax.axis_index("dp") >> bit) & 1) == 1


def cross(value, first, second):
    count = lax.axis_size("dp")
    flips = (1 << first, 1 << second)
    moves = [
        (2 * place + rank, 2 * (place ^ flips[rank]) + rank)
        for place in range(count)
        for rank in range(2)
    ]
    return lax.ppermute(value, ("dp", "tensor"), moves)


def pick(whole, place, axis):
    return lax.dynamic_index_in_dim(whole, place.astype(jnp.int32), axis, keepdims=False)


def total_of(keep, other, kind):
    return (keep.astype(jnp.float32) + other.astype(jnp.float32)).astype(kind)


def low_gather(own, axis):
    even = lax.axis_index("tensor") == 0
    right, down = sides(0), sides(1)
    near = cross(own, 1, 0)
    far = cross(jnp.stack([own, near]), 0, 1)
    below = jnp.where(even, near, far[0])
    beside = jnp.where(even, far[0], near)
    top = (jnp.where(right, beside, own), jnp.where(right, own, beside))
    base = (jnp.where(right, far[1], below), jnp.where(right, below, far[1]))
    upper = jnp.stack([jnp.where(down, b, t) for t, b in zip(top, base)], axis=axis)
    lower = jnp.stack([jnp.where(down, t, b) for t, b in zip(top, base)], axis=axis)
    return jnp.stack([upper, lower], axis=axis)


def low_scatter(whole, axis, kind):
    even = lax.axis_index("tensor") == 0
    right, down = sides(0), sides(1)
    flat = whole.reshape(whole.shape[:axis] + (4,) + whole.shape[axis + 2 :])

    def share(across, along):
        places = (jnp.where(even, 2 * side + across, 2 * along + side) for side in range(2))
        return jnp.stack([pick(flat, place, axis) for place in places], axis=axis)

    keep = share(right.astype(jnp.int32), down.astype(jnp.int32))
    send = share(1 - right.astype(jnp.int32), 1 - down.astype(jnp.int32))
    half = total_of(keep, cross(send, 0, 1), whole.dtype)
    place = jnp.where(even, down, right)
    other = cross(pick(half, ~place, axis), 1, 0)
    return total_of(pick(half, place, axis), other, kind)


def gather_rows(piece, low_first=False):
    uppers = list(range(dp_bits() - 1, 1, -1))
    current = low_gather(piece, 0) if low_first else piece
    for count, bit in enumerate(uppers):
        other = swap(current, bit)
        upper = sides(bit)
        current = jnp.stack(
            [jnp.where(upper, other, current), jnp.where(upper, current, other)], axis=count
        )
    if not low_first:
        current = low_gather(current, len(uppers))
    return current.reshape((-1,) + piece.shape)


def scatter_rows(whole, low_first=True):
    bits = dp_bits()
    shape = whole.shape[1:]
    current = whole.reshape((2,) * bits + shape)
    if low_first:
        current = low_scatter(current, bits - 2, whole.dtype)
    for bit in range(2, bits):
        place = sides(bit)
        axis = bits - 1 - bit
        last = low_first and bit == bits - 1
        kind = jnp.float32 if last else whole.dtype
        other = swap(pick(current, ~place, axis), bit)
        current = total_of(pick(current, place, axis), other, kind)
    if not low_first:
        current = low_scatter(current, 0, jnp.float32)
    return current


def pair_gather(piece):
    other = pair_swap(piece)
    upper = lax.axis_index("tensor") == 1
    return jnp.concatenate(
        [jnp.where(upper, other, piece), jnp.where(upper, piece, other)], axis=0
    )


def pair_scatter(whole):
    half = whole.shape[0] // 2
    rank = lax.axis_index("tensor")
    keep = lax.dynamic_slice_in_dim(whole, rank * half, half, 0)
    send = lax.dynamic_slice_in_dim(whole, (1 - rank) * half, half, 0)
    return keep + pair_swap(send.astype(jnp.bfloat16)).astype(jnp.float32)


def gather_vectors(vectors):
    packed = jnp.concatenate(vectors)[None]
    packed = pair_gather(packed)
    whole = gather_rows(packed, low_first=True).reshape(-1, packed.shape[1])
    results, offset = [], 0
    for vector in vectors:
        size = vector.shape[0]
        results.append(whole[:, offset : offset + size].reshape(-1))
        offset += size
    return results


def scatter_vectors(wholes):
    devices = lax.axis_size("dp") * 2
    packed = jnp.concatenate([whole.reshape(devices, -1) for whole in wholes], axis=1)
    columns = packed.shape[1]
    own = scatter_rows(packed.reshape(devices // 2, 2, columns), low_first=False)
    rank = lax.axis_index("tensor")
    own = pick(own, rank, 0) + pair_swap(pick(own, 1 - rank, 0))
    results, offset = [], 0
    for whole in wholes:
        size = whole.size // devices
        results.append(own[offset : offset + size])
        offset += size
    return tuple(results)


def lane_tables(offsets):
    half = RD // 2
    lanes = jnp.arange(LANES, dtype=jnp.int32) % HD
    frequency = jnp.power(10000.0, -2.0 * (lanes % half).astype(jnp.float32) / RD)
    angles = offsets.astype(jnp.float32)[:, None] * frequency[None, :]
    turned = (lanes < RD)[None, :]
    cosine = jnp.where(turned, jnp.cos(angles), 1.0)
    sine = jnp.sin(angles)
    ahead = jnp.where((lanes < half)[None, :], -sine, 0.0)
    behind = jnp.where((lanes >= half)[None, :] & turned, sine, 0.0)
    return (cosine, ahead, behind)


def product(left, right, left_axis, right_axis):
    return lax.dot_general(
        left,
        right,
        (((left_axis,), (right_axis,)), ((), ())),
        preferred_element_type=jnp.float32,
    )


def attention_kernel(
    attend_ref,
    upstream_ref,
    heads_ref,
    output_ref,
    bias_ref,
    cosine_ref,
    ahead_ref,
    behind_ref,
    segment_column_ref,
    segment_row_ref,
    branch_in_ref,
    heads_grad_ref,
    output_grad_ref,
    bias_grad_ref,
    branch_ref,
    attend_grad_ref,
    key_grad_ref,
    value_grad_ref,
):
    low = jnp.bfloat16
    rows = attend_ref.shape[0]
    local_width = heads_ref.shape[1] // 3
    scale = HD ** (-0.5)
    block = rows // 2
    branch_ref[...] = branch_in_ref[...]
    attend_grad_ref[...] = jnp.zeros_like(attend_grad_ref)

    def turn(value, sign):
        forward = pltpu.roll(value, LANES - RD // 2, 1) * ahead_ref[...]
        backward = pltpu.roll(value, RD // 2, 1) * behind_ref[...]
        return value * cosine_ref[...] + sign * (forward + backward)

    def one_pair(pair, carried):
        attend, upstream = attend_ref[...], upstream_ref[...]
        windows = [
            pl.ds(pl.multiple_of(which * local_width + pair * LANES, LANES), LANES)
            for which in range(3)
        ]
        band = pl.ds(pl.multiple_of(pair * LANES, LANES), LANES)

        def project(which):
            columns = windows[which]
            return product(attend, heads_ref[:, columns], 1, 0) + bias_ref[:, columns]

        query = (turn(project(0), 1.0).astype(low).astype(jnp.float32) * scale).astype(low)
        key = turn(project(1), 1.0).astype(low)
        value = project(2).astype(low)
        output_rows = output_ref[band, :]
        context_grad = product(upstream, output_rows, 1, 1).astype(low)
        key_grad_ref[...] = jnp.zeros_like(key_grad_ref)
        value_grad_ref[...] = jnp.zeros_like(value_grad_ref)
        contexts, query_grads = [], []
        for step in range(2):
            span = slice(step * block, (step + 1) * block)
            reach = (step + 1) * block
            same = segment_column_ref[span, :] == segment_row_ref[:, :reach]
            place = lax.broadcasted_iota(jnp.int32, (block, reach), 0) + step * block
            allowed = same & (place >= lax.broadcasted_iota(jnp.int32, (block, reach), 1))
            lanes = lax.broadcasted_iota(jnp.int32, (block, LANES), 1)
            context = jnp.zeros((block, LANES), jnp.float32)
            query_grad = jnp.zeros((block, LANES), jnp.float32)
            for head in range(LANES // HD):
                mine = (lanes >= head * HD) & (lanes < (head + 1) * HD)
                own_query = jnp.where(mine, query[span].astype(jnp.float32), 0.0).astype(low)
                own_grad = jnp.where(mine, context_grad[span].astype(jnp.float32), 0.0)
                own_grad = own_grad.astype(low)
                scores = jnp.where(allowed, product(own_query, key[:reach], 1, 1), NEG_LARGE)
                peak = jnp.max(scores, axis=1, keepdims=True)
                raised = jnp.exp(scores - peak)
                probs = raised * (1.0 / jnp.sum(raised, axis=1, keepdims=True))
                weights_low = probs.astype(low)
                context = jnp.where(mine, product(weights_low, value[:reach], 1, 0), context)
                prob_grad = product(own_grad, value[:reach], 1, 1)
                delta = jnp.sum(probs * prob_grad, axis=1, keepdims=True)
                score_grad = (probs * (prob_grad - delta)).astype(low)
                query_grad = jnp.where(
                    mine, product(score_grad, key[:reach], 1, 0), query_grad
                )
                key_grad_ref[:reach, :] += product(score_grad, own_query, 0, 0)
                value_grad_ref[:reach, :] += product(weights_low, own_grad, 0, 0)
            contexts.append(context.astype(low))
            query_grads.append(query_grad * scale)
        context_low = jnp.concatenate(contexts, axis=0)
        output_grad_ref[band, :] = product(context_low, upstream, 0, 0).astype(low)
        branch_ref[...] += product(context_low, output_rows, 1, 0)
        grads = (
            turn(jnp.concatenate(query_grads, axis=0), -1.0),
            turn(key_grad_ref[...], -1.0),
            value_grad_ref[...],
        )
        attend_grad = attend_grad_ref[...]
        for which, grad in enumerate(grads):
            columns = windows[which]
            bias_grad_ref[:, columns] = jnp.sum(grad, axis=0, keepdims=True)
            grad_low = grad.astype(low)
            heads_grad_ref[:, columns] = product(attend, grad_low, 0, 0).astype(low)
            attend_grad = attend_grad + product(grad_low, heads_ref[:, columns], 1, 1)
        attend_grad_ref[...] = attend_grad
        return carried

    lax.fori_loop(0, local_width // LANES, one_pair, 0)


def attention(operands, branch):
    rows, width = operands[0].shape
    local_width = operands[3].shape[0]
    low = jnp.bfloat16
    shapes = (
        ((width, 3 * local_width), low),
        ((local_width, width), low),
        ((1, 3 * local_width), jnp.float32),
        ((rows, width), jnp.float32),
        ((rows, width), jnp.float32),
    )
    space = pl.BlockSpec(memory_space=pltpu.VMEM)
    return pl.pallas_call(
        attention_kernel,
        out_shape=[jax.ShapeDtypeStruct(*each) for each in shapes],
        in_specs=[space] * (len(operands) + 1),
        out_specs=[space] * len(shapes),
        scratch_shapes=[pltpu.VMEM((rows, LANES), jnp.float32)] * 2,
        compiler_params=pltpu.CompilerParams(vmem_limit_bytes=12 * 1024 * 1024),
        cost_estimate=pl.CostEstimate(
            flops=48 * rows * width * local_width, transcendentals=0, bytes_accessed=24 << 20
        ),
        name="attention",
    )(*operands, branch)


def on_device(
    block_input,
    cotangent,
    segment_ids,
    positions,
    heads_weight,
    heads_weight_first,
    heads_weight_second,
    output_weight,
    output_weight_first,
    output_weight_second,
    expand_weight,
    expand_weight_first,
    expand_weight_second,
    shrink_weight,
    shrink_weight_first,
    shrink_weight_second,
    attention_gain,
    attention_gain_first,
    attention_gain_second,
    attention_shift,
    attention_shift_first,
    attention_shift_second,
    feedforward_gain,
    feedforward_gain_first,
    feedforward_gain_second,
    feedforward_shift,
    feedforward_shift_first,
    feedforward_shift_second,
    heads_bias,
    heads_bias_first,
    heads_bias_second,
    output_bias,
    output_bias_first,
    output_bias_second,
    expand_bias,
    expand_bias_first,
    expand_bias_second,
    shrink_bias,
    shrink_bias_first,
    shrink_bias_second,
):
    tensor_rank = lax.axis_index("tensor")
    width = block_input.shape[1]
    local_width = heads_weight.shape[2]
    local_hidden = expand_weight.shape[1]
    low = jnp.bfloat16

    input_all = pair_gather(block_input)
    upstream_all = pair_gather(cotangent.astype(low))
    vectors = (
        attention_gain,
        attention_shift,
        feedforward_gain,
        feedforward_shift,
        heads_bias,
        output_bias,
        expand_bias,
        shrink_bias,
    )
    (
        gain_one,
        shift_one,
        gain_two,
        shift_two,
        heads_bias_all,
        output_bias_all,
        expand_bias_all,
        shrink_bias_all,
    ) = gather_vectors(vectors)
    expand_low = gather_rows(expand_weight.astype(low)).reshape(width, local_hidden)
    shrink_low = gather_rows(shrink_weight.astype(low)).reshape(local_hidden, width)
    heads_flat = heads_weight.astype(low).reshape(-1, 3 * local_width)
    short, tall = output_weight.shape[0], heads_flat.shape[0]
    packed = gather_rows(
        jnp.concatenate(
            [
                output_weight.astype(low),
                heads_flat[:, :width],
                jnp.concatenate([heads_flat[:short, width:], heads_flat[short:, width:]], axis=1),
            ],
            axis=0,
        ).reshape(-1, short, width),
    )
    packed = packed.reshape(packed.shape[0], -1, width)
    output_low = packed[:, :short].reshape(local_width, width)
    thirds = packed[:, short + tall :]
    thirds = jnp.concatenate([thirds[..., :local_width], thirds[..., local_width:]], axis=1)
    heads_low = jnp.concatenate([packed[:, short : short + tall], thirds], axis=2)
    heads_low = heads_low.reshape(width, 3 * local_width)

    heads_bias_local = lax.dynamic_slice_in_dim(
        heads_bias_all.reshape(3, width), tensor_rank * local_width, local_width, 1
    )
    expand_bias_local = lax.dynamic_slice_in_dim(
        expand_bias_all, tensor_rank * local_hidden, local_hidden, 0
    )
    normalised, inverse = layer_statistics(block_input)
    normalised_all, _ = layer_statistics(input_all)
    attend_input = (normalised_all * gain_one + shift_one).astype(low)
    feed_input = (normalised_all * gain_two + shift_two).astype(low)

    expanded = (
        jnp.dot(feed_input, expand_low, preferred_element_type=jnp.float32) + expand_bias_local
    )
    activated = gelu_value(expanded).astype(low)
    shrink_grad = jnp.dot(activated.T, upstream_all, preferred_element_type=jnp.float32)
    shrink_own = scatter_rows(shrink_grad.astype(low).reshape((-1,) + shrink_weight.shape))
    expanded_grad = jnp.dot(
        upstream_all, shrink_low.T, preferred_element_type=jnp.float32
    ) * gelu_slope(expanded)
    expanded_low = expanded_grad.astype(low)
    expand_grad = jnp.dot(feed_input.T, expanded_low, preferred_element_type=jnp.float32)
    expand_own = scatter_rows(expand_grad.astype(low).reshape((-1,) + expand_weight.shape))
    feed_grad = jnp.dot(expanded_low, expand_low.T, preferred_element_type=jnp.float32)
    feed_own = pair_scatter(feed_grad)

    branch = jnp.dot(activated, shrink_low, preferred_element_type=jnp.float32)
    operands = (
        attend_input,
        upstream_all,
        heads_low,
        output_low,
        heads_bias_local.reshape(1, 3 * local_width),
        *lane_tables(positions),
        segment_ids[:, None],
        segment_ids[None, :],
    )
    heads_grad, output_grad, bias_grad, branch, attend_grad = attention(operands, branch)
    heads_bias_sum = bias_grad.reshape(3, local_width)
    attend_own = pair_scatter(attend_grad)
    block_output = block_input + pair_scatter(branch) + output_bias_all + shrink_bias_all
    tail = heads_grad[:, width:].reshape(-1, tall, local_width)
    packed = scatter_rows(
        jnp.concatenate(
            [
                output_grad.reshape(-1, short, width),
                heads_grad[:, :width].reshape(-1, tall, width),
                jnp.concatenate([tail[:, :short], tail[:, short:]], axis=2),
            ],
            axis=1,
        ),
    )
    output_own = packed[:short]
    thirds = packed[short + tall :]
    thirds = jnp.concatenate([thirds[:, :local_width], thirds[:, local_width:]], axis=0)
    heads_own = jnp.concatenate([packed[short : short + tall], thirds], axis=1)
    heads_own = heads_own.reshape(heads_weight.shape)

    gain_sums = (
        jnp.sum(attend_own * normalised, axis=0),
        jnp.sum(attend_own, axis=0),
        jnp.sum(feed_own * normalised, axis=0),
        jnp.sum(feed_own, axis=0),
    )
    direct = attend_own * gain_one + feed_own * gain_two
    input_gradient = cotangent + inverse * (
        direct
        - jnp.mean(direct, axis=1, keepdims=True)
        - normalised * jnp.mean(direct * normalised, axis=1, keepdims=True)
    )
    heads_bias_part = lax.dynamic_update_slice_in_dim(
        jnp.zeros((3, width), jnp.float32), heads_bias_sum, tensor_rank * local_width, 1
    ).reshape(3 * width)
    expand_bias_part = lax.dynamic_update_slice_in_dim(
        jnp.zeros((expand_bias_all.shape[0],), jnp.float32),
        jnp.sum(expanded_grad, axis=0),
        tensor_rank * local_hidden,
        0,
    )
    upstream_sum = jnp.sum(cotangent, axis=0)
    matrix_grads = (heads_own, output_own, expand_own, shrink_own)
    vector_grads = scatter_vectors(
        gain_sums + (heads_bias_part, upstream_sum, expand_bias_part, upstream_sum)
    )
    params = (
        heads_weight,
        output_weight,
        expand_weight,
        shrink_weight,
        attention_gain,
        attention_shift,
        feedforward_gain,
        feedforward_shift,
        heads_bias,
        output_bias,
        expand_bias,
        shrink_bias,
    )
    firsts = (
        heads_weight_first,
        output_weight_first,
        expand_weight_first,
        shrink_weight_first,
        attention_gain_first,
        attention_shift_first,
        feedforward_gain_first,
        feedforward_shift_first,
        heads_bias_first,
        output_bias_first,
        expand_bias_first,
        shrink_bias_first,
    )
    seconds = (
        heads_weight_second,
        output_weight_second,
        expand_weight_second,
        shrink_weight_second,
        attention_gain_second,
        attention_shift_second,
        feedforward_gain_second,
        feedforward_shift_second,
        heads_bias_second,
        output_bias_second,
        expand_bias_second,
        shrink_bias_second,
    )
    gradients = tuple(matrix_grads) + tuple(vector_grads)
    results = [block_output, input_gradient]
    for number in range(12):
        params, firsts, seconds, gradients = (
            each[:number] + (value,) + each[number + 1 :]
            for each, value in zip(
                (params, firsts, seconds, gradients),
                lax.optimization_barrier(
                    (params[number], firsts[number], seconds[number], gradients[number])
                ),
            )
        )
        decay = DECAY if number < 4 else 0.0
        param_next, first_next, second_next = adamw(
            params[number], firsts[number], seconds[number], gradients[number], decay
        )
        results.extend([gradients[number], param_next, first_next, second_next])
    return tuple(results)


def solution(mesh):
    both = ("dp", "tensor")
    tokens, shards = P(both, None), P(both)
    heads, expands = P("dp", None, "tensor"), P("dp", "tensor")
    stacked = P(("tensor", "dp"), None)
    matrices = (heads, stacked, expands, stacked)
    in_specs = (tokens, tokens, P("dp"), P("dp"))
    in_specs += tuple(spec for spec in matrices for _ in range(3)) + (shards,) * 24
    out_specs = (tokens, tokens)
    out_specs += tuple(spec for spec in matrices for _ in range(4)) + (shards,) * 32
    return jax.shard_map(
        on_device, mesh=mesh, in_specs=in_specs, out_specs=out_specs, check_vma=False
    )
```
